32 devices in a mesh: groups: 2 (over y), seq: 16 (over z, x, core).
Axes of the slice: x: 2, y: 2, z: 4, core: 2. Of those that a mesh axis runs over, the one named last changes fastest.
Arguments:
- frames_in: bfloat16 [8192, 1024], P(('groups', 'seq')), parts along dimension 0, may hold values from -40 to 40
- rec_start: int32 [8192], P(('groups', 'seq')), parts along dimension 0, may hold values from 0 to 4095, as said below
- norm_attn: float32 [1024], replicated, may hold values from 0.1 to 1.9
- w_query: bfloat16 [1024, 1024], replicated, may hold values from -1 to 1
- w_key: bfloat16 [1024, 1024], replicated, may hold values from -1 to 1
- w_value: bfloat16 [1024, 1024], replicated, may hold values from -0.1875 to 0.1875
- w_out: bfloat16 [1024, 1024], replicated, may hold values from -0.1875 to 0.1875
- norm_conv: float32 [1024], replicated, may hold values from 0.1 to 1.9
- w_glu: bfloat16 [1024, 2048], replicated, may hold values from -0.1875 to 0.1875
- w_depth: float32 [31, 1024], replicated, may hold values from -1 to 1
- norm_depth: float32 [1024], replicated, may hold values from 0.1 to 1.9
Outputs:
- conv_out: bfloat16 [8192, 1024], P(('groups', 'seq')), parts along dimension 0
The draws below stay inside these ranges and needn't reach their ends.
There are 2 independent parts, one for each index of `groups`. The reference program is written for one: setup_inputs(seed, part) draws one part's arguments, and reference() takes and returns one part's arrays. A program takes and returns all parts, laid end to end along the dimension named above; an argument that names none is the same for every part. Nothing has to cross between parts.
Inputs may be any that keep to these rules, and one draw needn't show every extreme that they name: Recordings lie end to end from frame 0; rec_start[i] is the first frame of the recording that holds frame i. Each recording has 213 to 1280 frames, except the last, which the slab's end may cut; one of the first two has exactly 1280 frames.
All inputs are finite; a program needn't handle non-finite values.
Results may differ from the reference program's by a relative error of at most 0.0065.
Values may be sent and summed in bfloat16 or wider, within the bound.
A program may use at most 128 MiB of HBM per device.

```python
import math
import jax
import jax.numpy as jnp
from jax import lax

D = 1024
HD = 64
KW = 31
FRAMES = 256
HOPS = 5
REC_MAX = 1280
REC_MIN = 213
SLAB = 4096


LOG_TEN = 2.302585092994046


def draw_frames_in(key, part):
    key_base, key_rows, key_columns = jax.random.split(jax.random.fold_in(key, 3), 3)
    base = jax.random.truncated_normal(key_base, -4.0, 4.0, (SLAB, D), jnp.float32)
    row_scale = jnp.exp(jax.random.uniform(key_rows, (SLAB, 1), jnp.float32, 0.0, LOG_TEN))
    column_scale = jnp.exp(jax.random.uniform(key_columns, (1, D), jnp.float32, 0.0, LOG_TEN))
    return jnp.clip(base * row_scale * column_scale / 10.0, -40.0, 40.0).astype(jnp.bfloat16)


def projection_pair(key):
    key_first, key_second = jax.random.split(jax.random.fold_in(key, 101), 2)
    spread = (4.0 / D) ** 0.5
    first_matrix = jax.random.truncated_normal(key_first, -4.0, 4.0, (D, D), jnp.float32) * spread
    second_matrix = jax.random.truncated_normal(key_second, -4.0, 4.0, (D, D), jnp.float32) * spread
    return (jnp.clip(first_matrix, -1.0, 1.0), jnp.clip(second_matrix, -1.0, 1.0))


def draw_w_query(key, part):
    return projection_pair(key)[0].astype(jnp.bfloat16)


def draw_w_key(key, part):
    return projection_pair(key)[1].astype(jnp.bfloat16)


def draw_rec_start(key, part):
    record_count = SLAB // REC_MIN + 2
    key_lengths, key_longest = jax.random.split(jax.random.fold_in(key, 7))
    lengths = jax.random.randint(key_lengths, (record_count,), REC_MIN, REC_MAX + 1, jnp.int32)
    longest = jax.random.randint(key_longest, (), 0, 2, jnp.int32)
    lengths = jnp.where(jnp.arange(record_count, dtype=jnp.int32) == longest, REC_MAX, lengths)
    record_ends = jnp.cumsum(lengths)
    record_begins = record_ends - lengths
    places = jnp.arange(SLAB, dtype=jnp.int32)
    record_index = jnp.sum((record_ends[None, :] <= places[:, None]).astype(jnp.int32), axis=1)
    chosen = jnp.arange(record_count, dtype=jnp.int32)[None, :] == record_index[:, None]
    return jnp.sum(jnp.where(chosen, record_begins[None, :], 0), axis=1).astype(jnp.int32)


def bell_draw(key, extent, scale, most, kind=jnp.bfloat16):
    values = scale * jax.random.normal(key, extent, jnp.float32)
    return jnp.clip(values, min=-most, max=most).astype(kind)


def setup_inputs(seed: int = 0, part: int = 0) -> dict:
    splits = jax.random.split(jax.random.key(seed), 12)
    part_splits = jax.random.split(jax.random.fold_in(splits[11], part), 12)
    frames_in = draw_frames_in(jax.random.fold_in(jax.random.fold_in(splits[11], part), 71), part)
    rec_start = draw_rec_start(jax.random.fold_in(jax.random.fold_in(splits[11], part), 71), part)
    norm_attn = jnp.clip(1.0 + 0.18 * jax.random.normal(splits[2], (D,), jnp.float32), 0.1, 1.9)
    w_query = draw_w_query(jax.random.fold_in(splits[11], 71), part)
    w_key = draw_w_key(jax.random.fold_in(splits[11], 71), part)
    w_value = bell_draw(splits[5], (D, D), D ** -0.5, 0.1875)
    w_out = bell_draw(splits[6], (D, D), D ** -0.5, 0.1875)
    norm_conv = jnp.clip(1.0 + 0.18 * jax.random.normal(splits[7], (D,), jnp.float32), 0.1, 1.9)
    w_glu = bell_draw(splits[8], (D, 2 * D), D ** -0.5, 0.1875)
    w_depth = bell_draw(splits[9], (KW, D), KW ** -0.5, 1.0, jnp.float32)
    norm_depth = jnp.clip(1.0 + 0.18 * jax.random.normal(splits[10], (D,), jnp.float32), 0.1, 1.9)
    return {"frames_in": frames_in, "rec_start": rec_start, "norm_attn": norm_attn, "w_query": w_query, "w_key": w_key, "w_value": w_value, "w_out": w_out, "norm_conv": norm_conv, "w_glu": w_glu, "w_depth": w_depth, "norm_depth": norm_depth}


EPSILON = 1e-05
FLOOR_SCORE = -1e+30

def layer_norm(entries, scaling):
    entries = entries.astype(jnp.float32)
    center = entries - lax.optimization_barrier(jnp.mean(entries, axis=-1, keepdims=True))
    spread = lax.optimization_barrier(jnp.mean(center * center, axis=-1, keepdims=True))
    return center * lax.rsqrt(spread + EPSILON) * scaling.astype(jnp.float32)

def gated_units(features, norm_conv, w_glu):
    normed_conv = layer_norm(features, norm_conv).astype(jnp.bfloat16)
    mixed = jnp.dot(normed_conv, w_glu, preferred_element_type=jnp.float32)
    feature_width = features.shape[1]
    return (mixed[:, :feature_width] * jax.nn.sigmoid(mixed[:, feature_width:])).astype(jnp.bfloat16)

def reference(frames_in, rec_start, norm_attn, w_query, w_key, w_value, w_out, norm_conv, w_glu, w_depth, norm_depth):
    head_count = D // HD
    normed_in = layer_norm(frames_in, norm_attn).astype(jnp.bfloat16)
    query = jnp.dot(normed_in, w_query, preferred_element_type=jnp.float32).astype(jnp.bfloat16)
    key_rows = jnp.dot(normed_in, w_key, preferred_element_type=jnp.float32).astype(jnp.bfloat16)
    value_rows = jnp.dot(normed_in, w_value, preferred_element_type=jnp.float32).astype(jnp.bfloat16)
    reach = HOPS * FRAMES
    window = reach + FRAMES
    front_zeros = jnp.zeros((reach, D), jnp.bfloat16)
    keys_long = jnp.concatenate([front_zeros, key_rows], axis=0)
    values_long = jnp.concatenate([front_zeros, value_rows], axis=0)
    score_scale = 1.0 / math.sqrt(HD)

    def attend_block(block_index):
        begin = block_index * FRAMES
        query_heads = lax.dynamic_slice_in_dim(query, begin, FRAMES, 0).astype(jnp.float32).reshape(FRAMES, head_count, HD)
        key_heads = lax.dynamic_slice_in_dim(keys_long, begin, window, 0).astype(jnp.float32).reshape(window, head_count, HD)
        value_heads = lax.dynamic_slice_in_dim(values_long, begin, window, 0).astype(jnp.float32).reshape(window, head_count, HD)
        starts = lax.dynamic_slice_in_dim(rec_start, begin, FRAMES, 0)
        query_places = begin + jnp.arange(FRAMES, dtype=jnp.int32)
        key_places = begin - reach + jnp.arange(window, dtype=jnp.int32)
        visible = (key_places[None, :] >= starts[:, None]) & (key_places[None, :] <= query_places[:, None])
        scores = jnp.einsum('qhd,khd->hqk', query_heads, key_heads) * score_scale
        highest = lax.optimization_barrier(jnp.max(jnp.where(visible[None], scores, FLOOR_SCORE), axis=-1, keepdims=True))
        weights = jnp.where(visible[None], jnp.exp(scores - highest), 0.0).astype(jnp.bfloat16)
        weight_sum = lax.optimization_barrier(jnp.sum(weights.astype(jnp.float32), axis=-1))
        summed = jnp.einsum('hqk,khd->qhd', weights.astype(jnp.float32), value_heads)
        return (summed / weight_sum.T[:, :, None]).reshape(FRAMES, D).astype(jnp.bfloat16)
    heads_out = lax.map(attend_block, jnp.arange(SLAB // FRAMES, dtype=jnp.int32)).reshape(SLAB, D)
    attn_res = (frames_in.astype(jnp.float32) + jnp.dot(heads_out, w_out, preferred_element_type=jnp.float32)).astype(jnp.bfloat16)
    gated = gated_units(attn_res, norm_conv, w_glu)
    padded = jnp.concatenate([jnp.zeros((KW - 1, D), jnp.bfloat16), gated], axis=0)
    places = jnp.arange(SLAB, dtype=jnp.int32)
    depth = jnp.zeros((SLAB, D), jnp.float32)
    for tap_index in range(KW):
        source = places - (KW - 1) + tap_index
        keep = (source >= rec_start)[:, None]
        depth = depth + jnp.where(keep, padded[tap_index:tap_index + SLAB].astype(jnp.float32), 0.0) * w_depth[tap_index].astype(jnp.float32)
    normed_depth = layer_norm(depth, norm_depth)
    return (attn_res.astype(jnp.float32) + normed_depth * jax.nn.sigmoid(normed_depth)).astype(jnp.bfloat16)
```

```python
import jax
import jax.numpy as jnp
from jax import lax
from jax.experimental import pallas as pl
from jax.experimental.pallas import tpu as pltpu
from jax.sharding import PartitionSpec as P

HD = 64
KW = 31
EPSILON = 1e-05
FLOOR_SCORE = -1e30
F32 = jnp.float32
BF16 = jnp.bfloat16
MESH = pl.DeviceIdType.MESH
PIECES = 2
PLACE = {4: 0, 2: 1, 1: 2, 3: 3, 5: 4}
DISTANCE = (4, 2, 1, 3, 5)
A, B, C, D, E, F, G, H, I = range(9)


def layer_norm(entries, scaling):
    center = entries - jnp.mean(entries, axis=-1, keepdims=True)
    spread = jnp.mean(center * center, axis=-1, keepdims=True)
    return center * lax.rsqrt(spread + EPSILON) * scaling


def kernel(
    x_ref, start_ref, na_ref, nc_ref, nd_ref, wd_ref,
    wq_hbm, wk_hbm, wv_hbm, wo_hbm, wg_hbm,
    out_ref,
    xb, wq, wk, wv, wo, wg, xn, q2, kb, vb, bias, bias_own, startb, mx, acc, heads,
    res, gb, halo, gext, depth,
    w_sem, send_sem, recv_sem, halo_sem,
):
    n = lax.axis_size("seq")
    me = lax.axis_index("seq")
    p = me % 4
    rows, width = x_ref.shape
    piece = rows // PIECES
    pairs = width // 128

    barrier = pltpu.get_barrier_semaphore()
    peers = jnp.int32(0)
    for delta in (-4, -3, -2, -1, 1, 2, 3, 4):
        inside = (me + delta >= 0) & (me + delta < n)
        peers = peers + jnp.where(inside, 1, 0)

        @pl.when(inside)
        def _():
            pl.semaphore_signal(
                barrier, inc=1, device_id={"seq": me + delta}, device_id_type=MESH
            )
    pl.semaphore_wait(barrier, peers)

    def move(event, part, source, target, distance):
        span = pl.ds(part * piece, piece)
        src = x_ref.at[span] if source is None else xb.at[PLACE[source], span]
        return pltpu.make_async_remote_copy(
            src_ref=src,
            dst_ref=xb.at[PLACE[distance], span],
            send_sem=send_sem.at[event, part],
            recv_sem=recv_sem.at[event, part],
            device_id={"seq": target},
            device_id_type=MESH,
        )

    even = p % 2 == 0
    sends = {
        A: [(me + 4 < n, None, me + 4, 4)],
        B: [(p < 2, None, me + 2, 2)],
        C: [(even, None, me + 1, 1)],
        D: [(p == 2, 2, me + 1, 3), (p == 3, 2, me - 1, 1)],
        E: [((me >= 4) & even, 4, me + 1, 5), ((me >= 4) & (p % 2 == 1), 4, me - 1, 3)],
        F: [((me >= 4) & (p >= 2), 4, me - 2, 2)],
        G: [((me >= 4) & (p == 0), 2, me + 1, 3), ((me >= 4) & (p == 1), 2, me - 1, 1)],
        H: [((p == 3) & (me + 3 < n), 2, me + 3, 5)],
        I: [((me >= 4) & (p == 1) & (me + 3 < n), 2, me + 3, 5)],
    }
    receipts = {
        A: [(me >= 4, 4)],
        B: [(p >= 2, 2)],
        C: [(p % 2 == 1, 1)],
        D: [(p == 3, 3), (p == 2, 1)],
        E: [((me >= 4) & (p % 2 == 1), 5), ((me >= 4) & even, 3)],
        F: [((me >= 4) & (p < 2), 2)],
        G: [((me >= 4) & (p == 1), 3), ((me >= 4) & (p == 0), 1)],
        H: [((me >= 4) & (p == 2), 5)],
        I: [((me >= 8) & (p == 0), 5)],
    }

    def start(event, part):
        for condition, source, target, distance in sends[event]:
            @pl.when(condition)
            def _():
                move(event, part, source, target, distance).start()

    def wait_sent(event, part):
        for condition, source, target, distance in sends[event]:
            @pl.when(condition)
            def _():
                move(event, part, source, target, distance).wait_send()

    def wait_here(event, part):
        for condition, distance in receipts[event]:
            @pl.when(condition)
            def _():
                move(event, part, None, me, distance).wait_recv()

    for part in range(PIECES):
        start(A, part)
        start(B, part)
    for part in range(PIECES):
        start(C, part)

    weights = [
        pltpu.make_async_copy(src, dst, w_sem.at[index])
        for index, (src, dst) in enumerate(
            ((wq_hbm, wq), (wk_hbm, wk), (wv_hbm, wv), (wo_hbm, wo), (wg_hbm, wg))
        )
    ]
    for copy in weights:
        copy.start()

    for distance in DISTANCE:
        @pl.when(me < distance)
        def _():
            xb[PLACE[distance]] = jnp.zeros((rows, width), BF16)

    column = jnp.broadcast_to(start_ref[...].astype(F32), (rows, rows)).T
    startb[...] = column[:, :128] - (me * rows).astype(F32)
    first = startb[...]
    lane = lax.broadcasted_iota(jnp.int32, (rows, 128), 1).astype(F32)
    row_index = lax.broadcasted_iota(jnp.int32, (rows, 128), 0).astype(F32)
    for tile in range(rows // 128):
        place = lane + float(tile * 128)
        seen = (place >= first) & (place <= row_index)
        bias_own[:, tile * 128:(tile + 1) * 128] = jnp.where(seen, 0.0, FLOOR_SCORE)
        for slot, distance in enumerate(DISTANCE):
            at = slot * rows + tile * 128
            bias[:, at:at + 128] = jnp.where(
                place - float(distance * rows) >= first, 0.0, FLOOR_SCORE
            )

    def key_values(count):
        def column_tile(index, carry):
            cols = pl.ds(pl.multiple_of(index * 256, 256), 256)
            normed = xn[0:count * rows, :]
            kb[0:count * rows, cols] = jnp.dot(
                normed, wk[:, cols], preferred_element_type=F32
            ).astype(BF16)
            vb[0:count * rows, cols] = jnp.dot(
                normed, wv[:, cols], preferred_element_type=F32
            ).astype(BF16)
            return carry

        lax.fori_loop(0, width // 256, column_tile, 0)

    def attend(count, bias_view, opening):
        keys = count * rows

        def pair_step(pair, carry):
            cols = pl.ds(pl.multiple_of(pair * 128, 128), 128)
            shade = bias_view()
            scores = lax.dot_general(
                q2[:, cols], kb[0:keys, cols], (((1,), (1,)), ((), ())),
                preferred_element_type=F32,
            ) + jnp.concatenate([shade, shade], axis=0)
            top = jnp.broadcast_to(
                jnp.max(scores, axis=-1, keepdims=True), (2 * rows, 128)
            )
            if not opening:
                before = mx[pair]
                top = jnp.maximum(top, before)
            weights16 = jnp.exp(scores - jnp.tile(top, (1, keys // 128))).astype(BF16)
            values = jnp.concatenate(
                [vb[0:keys, cols], jnp.ones((keys, 128), BF16)], axis=1
            )
            summed = jnp.dot(weights16, values, preferred_element_type=F32)
            if not opening:
                summed = summed + acc[pair] * jnp.tile(jnp.exp(before - top), (1, 2))
            acc[pair] = summed
            mx[pair] = top
            return carry

        lax.fori_loop(0, pairs, pair_step, 0)

    gain = na_ref[...]
    xn[0:rows, :] = layer_norm(x_ref[...].astype(F32), gain).astype(BF16)

    weights[0].wait()

    def query_tile(index, carry):
        cols = pl.ds(pl.multiple_of(index * 256, 256), 256)
        query = jnp.dot(xn[0:rows, :], wq[:, cols], preferred_element_type=F32)
        query = query.astype(BF16).astype(F32) * (HD ** -0.5)
        low = lax.broadcasted_iota(jnp.int32, (rows, 256), 1) % 128 < HD
        q2[0:rows, cols] = jnp.where(low, query, 0.0).astype(BF16)
        q2[rows:2 * rows, cols] = jnp.where(low, 0.0, query).astype(BF16)
        return carry

    lax.fori_loop(0, width // 256, query_tile, 0)
    weights[1].wait()
    weights[2].wait()
    key_values(1)

    def relay_first(part):
        wait_here(B, part)
        start(D, part)
        start(H, part)
        wait_here(A, part)
        start(F, part)
        start(E, part)

    def relay_second(part):
        wait_here(F, part)
        start(I, part)
        start(G, part)

    attend(1, lambda: bias_own[...], True)
    for part in range(PIECES):
        relay_first(part)

    def remote(slot, count):
        for index in range(count):
            xn[index * rows:(index + 1) * rows, :] = layer_norm(
                xb[slot + index].astype(F32), gain
            ).astype(BF16)
        key_values(count)
        attend(count, lambda: bias[:, slot * rows:(slot + count) * rows], False)

    remote(0, 1)
    for part in range(PIECES):
        relay_second(part)
    remote(1, 1)
    for event in (C, D, E, G, H, I):
        for part in range(PIECES):
            wait_here(event, part)
    remote(2, 3)

    low = lax.broadcasted_iota(jnp.int32, (rows, 128), 1) < HD

    def close_pair(pair, carry):
        cols = pl.ds(pl.multiple_of(pair * 128, 128), 128)
        state = acc[pair]
        total = jnp.where(low, state[0:rows, 0:128], state[rows:2 * rows, 0:128])
        weight_sum = jnp.where(low, state[0:rows, 128:256], state[rows:2 * rows, 128:256])
        heads[:, cols] = (total / weight_sum).astype(BF16)
        return carry

    lax.fori_loop(0, pairs, close_pair, 0)
    weights[3].wait()

    def output_tile(index, carry):
        cols = pl.ds(pl.multiple_of(index * 256, 256), 256)
        res[:, cols] = (
            x_ref[:, cols].astype(F32)
            + jnp.dot(heads[...], wo[:, cols], preferred_element_type=F32)
        ).astype(BF16)
        return carry

    lax.fori_loop(0, width // 256, output_tile, 0)
    xn[0:rows, :] = layer_norm(res[...].astype(F32), nc_ref[...]).astype(BF16)
    weights[4].wait()

    def unit_tile(index, carry):
        cols = pl.ds(pl.multiple_of(index * 256, 256), 256)
        gate_cols = pl.ds(pl.multiple_of(width + index * 256, 256), 256)
        normed = xn[0:rows, :]
        value = jnp.dot(normed, wg[:, cols], preferred_element_type=F32)
        gate = jnp.dot(normed, wg[:, gate_cols], preferred_element_type=F32)
        gated = (value * jax.nn.sigmoid(gate)).astype(BF16)
        gb[:, cols] = gated
        gext[32:32 + rows, cols] = gated.astype(F32)
        return carry

    lax.fori_loop(0, width // 256, unit_tile, 0)

    rim = pltpu.make_async_remote_copy(
        src_ref=gb.at[pl.ds(rows - 32, 32)],
        dst_ref=halo,
        send_sem=halo_sem.at[0],
        recv_sem=halo_sem.at[1],
        device_id={"seq": me + 1},
        device_id_type=MESH,
    )

    @pl.when(me + 1 < n)
    def _():
        rim.start()

    chunk = 64

    def depth_tile(base, cols):
        back = (
            lax.broadcasted_iota(jnp.int32, (chunk, 128), 0).astype(F32) + float(base)
            - startb[pl.ds(base, chunk), :]
        )
        total = jnp.zeros((chunk, 128), F32)
        for tap in range(KW):
            piece_rows = gext[pl.ds(base + 2 + tap, chunk), cols]
            kept = jnp.where(back >= float(KW - 1 - tap), piece_rows, 0.0)
            total = total + kept * wd_ref[tap:tap + 1, cols]
        depth[pl.ds(base, chunk), cols] = total

    def interior(index, carry):
        cols = pl.ds(pl.multiple_of(index * 128, 128), 128)
        for base in range(chunk, rows, chunk):
            depth_tile(base, cols)
        return carry

    lax.fori_loop(0, pairs, interior, 0)

    def finish(low_row, count):
        normed_depth = layer_norm(depth[low_row:low_row + count, :], nd_ref[...])
        out_ref[low_row:low_row + count, :] = (
            res[low_row:low_row + count, :].astype(F32)
            + normed_depth * jax.nn.sigmoid(normed_depth)
        ).astype(BF16)

    finish(chunk, rows - chunk)

    @pl.when(me == 0)
    def _():
        halo[...] = jnp.zeros_like(halo)

    @pl.when(me > 0)
    def _():
        rim.wait_recv()

    gext[0:32, :] = halo[...].astype(F32)

    def edge(index, carry):
        depth_tile(0, pl.ds(pl.multiple_of(index * 128, 128), 128))
        return carry

    lax.fori_loop(0, pairs, edge, 0)
    finish(0, chunk)

    for event in range(9):
        for part in range(PIECES):
            wait_sent(event, part)

    @pl.when(me + 1 < n)
    def _():
        rim.wait_send()


def body(
    frames_in, rec_start, norm_attn, w_query, w_key, w_value, w_out, norm_conv, w_glu, w_depth,
    norm_depth,
):
    rows, width = frames_in.shape
    pairs = width // 128
    vmem = pl.BlockSpec(memory_space=pltpu.VMEM)
    hbm = pl.BlockSpec(memory_space=pl.ANY)
    square = pltpu.VMEM((width, width), BF16)
    return pl.pallas_call(
        kernel,
        out_shape=jax.ShapeDtypeStruct((rows, width), BF16),
        in_specs=[vmem] * 6 + [hbm] * 5,
        out_specs=vmem,
        scratch_shapes=[
            pltpu.VMEM((5, rows, width), BF16),
            square, square, square, square,
            pltpu.VMEM((width, 2 * width), BF16),
            pltpu.VMEM((3 * rows, width), BF16),
            pltpu.VMEM((2 * rows, width), BF16),
            pltpu.VMEM((3 * rows, width), BF16),
            pltpu.VMEM((3 * rows, width), BF16),
            pltpu.VMEM((rows, 5 * rows), F32),
            pltpu.VMEM((rows, rows), F32),
            pltpu.VMEM((rows, 128), F32),
            pltpu.VMEM((pairs, 2 * rows, 128), F32),
            pltpu.VMEM((pairs, 2 * rows, 256), F32),
            pltpu.VMEM((rows, width), BF16),
            pltpu.VMEM((rows, width), BF16),
            pltpu.VMEM((rows, width), BF16),
            pltpu.VMEM((32, width), BF16),
            pltpu.VMEM((rows + 32, width), F32),
            pltpu.VMEM((rows, width), F32),
            pltpu.SemaphoreType.DMA((5,)),
            pltpu.SemaphoreType.DMA((9, PIECES)),
            pltpu.SemaphoreType.DMA((9, PIECES)),
            pltpu.SemaphoreType.DMA((2,)),
        ],
        compiler_params=pltpu.CompilerParams(
            collective_id=0, has_side_effects=True, vmem_limit_bytes=60 * 1024 * 1024
        ),
    )(
        frames_in, rec_start.reshape(1, rows), norm_attn.reshape(1, width),
        norm_conv.reshape(1, width), norm_depth.reshape(1, width), w_depth,
        w_query, w_key, w_value, w_out, w_glu,
    )


def solution(mesh):
    return jax.shard_map(
        body,
        mesh=mesh,
        in_specs=(P(("groups", "seq"), None), P(("groups", "seq"))) + (P(),) * 9,
        out_specs=P(("groups", "seq"), None),
        check_vma=False,
    )
```

```python
import jax
import jax.numpy as jnp
from jax import lax
from jax.experimental import pallas as pl
from jax.experimental.pallas import tpu as pltpu
from jax.sharding import PartitionSpec as P

HD = 64
KW = 31
EPSILON = 1e-05
FLOOR_SCORE = -1e30
F32 = jnp.float32
BF16 = jnp.bfloat16
MESH = pl.DeviceIdType.MESH
PIECES = 2
UNROLL = 4
TILE = 512
GROUPS = ((0, 1), (1, 1), (2, 3))
PLACE = {4: 0, 2: 1, 1: 2, 3: 3, 5: 4}
DISTANCE = (4, 2, 1, 3, 5)
A, B, C, D, E, F, G, H, I = range(9)


def layer_norm(entries, scaling):
    center = entries - jnp.mean(entries, axis=-1, keepdims=True)
    spread = jnp.mean(center * center, axis=-1, keepdims=True)
    return center * lax.rsqrt(spread + EPSILON) * scaling


def kernel(
    x_ref, start_ref, na_ref, nc_ref, nd_ref, wd_ref,
    wq_hbm, wk_hbm, wv_hbm, wo_hbm, wg_hbm,
    out_ref,
    xb, own, qx, kx, wq, wk, wv, wo, wg, xn, q2, kb, vb, bias_own, startb, mx, acc, heads,
    res, gb, halo, gext, depth,
    w_sem, send_sem, recv_sem, halo_sem,
):
    n = lax.axis_size("seq")
    me = lax.axis_index("seq")
    p = me % 4
    rows, width = x_ref.shape
    piece = rows // PIECES
    pairs = width // 128

    barrier = pltpu.get_barrier_semaphore()
    peers = jnp.int32(0)
    for delta in (-4, -3, -2, -1, 1, 2, 3, 4):
        inside = (me + delta >= 0) & (me + delta < n)
        peers = peers + jnp.where(inside, 1, 0)

        @pl.when(inside)
        def _():
            pl.semaphore_signal(
                barrier, inc=1, device_id={"seq": me + delta}, device_id_type=MESH
            )
    pl.semaphore_wait(barrier, peers)

    def move(event, part, source, target, distance):
        span = pl.ds(part * piece, piece)
        src = own.at[span] if source is None else xb.at[PLACE[source], span]
        return pltpu.make_async_remote_copy(
            src_ref=src,
            dst_ref=xb.at[PLACE[distance], span],
            send_sem=send_sem.at[event, part],
            recv_sem=recv_sem.at[event, part],
            device_id={"seq": target},
            device_id_type=MESH,
        )

    even = p % 2 == 0
    sends = {
        A: [(me + 4 < n, None, me + 4, 4)],
        B: [(p < 2, None, me + 2, 2)],
        C: [(even, None, me + 1, 1)],
        D: [(p == 2, 2, me + 1, 3), (p == 3, 2, me - 1, 1)],
        E: [((me >= 4) & even, 4, me + 1, 5), ((me >= 4) & (p % 2 == 1), 4, me - 1, 3)],
        F: [((me >= 4) & (p >= 2), 4, me - 2, 2)],
        G: [((me >= 4) & (p == 0), 2, me + 1, 3), ((me >= 4) & (p == 1), 2, me - 1, 1)],
        H: [((p == 3) & (me + 3 < n), 2, me + 3, 5)],
        I: [((me >= 4) & (p == 1) & (me + 3 < n), 2, me + 3, 5)],
    }
    receipts = {
        A: [(me >= 4, 4)],
        B: [(p >= 2, 2)],
        C: [(p % 2 == 1, 1)],
        D: [(p == 3, 3), (p == 2, 1)],
        E: [((me >= 4) & (p % 2 == 1), 5), ((me >= 4) & even, 3)],
        F: [((me >= 4) & (p < 2), 2)],
        G: [((me >= 4) & (p == 1), 3), ((me >= 4) & (p == 0), 1)],
        H: [((me >= 4) & (p == 2), 5)],
        I: [((me >= 8) & (p == 0), 5)],
    }

    def start(event, part):
        for condition, source, target, distance in sends[event]:
            @pl.when(condition)
            def _():
                move(event, part, source, target, distance).start()

    def wait_sent(event, part):
        for condition, source, target, distance in sends[event]:
            @pl.when(condition)
            def _():
                move(event, part, source, target, distance).wait_send()

    def wait_here(event, part):
        for condition, distance in receipts[event]:
            @pl.when(condition)
            def _():
                move(event, part, None, me, distance).wait_recv()

    weights = [
        pltpu.make_async_copy(src, dst, w_sem.at[index])
        for index, (src, dst) in enumerate(
            ((wq_hbm, wq), (wk_hbm, wk), (wv_hbm, wv), (wo_hbm, wo), (wg_hbm, wg))
        )
    ]
    for copy in weights:
        copy.start()

    gain = na_ref[...]
    for part in range(PIECES):
        own[part * piece:(part + 1) * piece, :] = layer_norm(
            x_ref[part * piece:(part + 1) * piece, :].astype(F32), gain
        ).astype(BF16)
        start(A, part)
        start(B, part)
    for part in range(PIECES):
        start(C, part)

    for distance in DISTANCE:
        @pl.when(me < distance)
        def _():
            xb[PLACE[distance]] = jnp.zeros((rows, width), BF16)

    column = jnp.broadcast_to(start_ref[...].astype(F32), (rows, rows)).T
    startb[...] = column[:, :128] - (me * rows).astype(F32)
    first = startb[...]
    lane = lax.broadcasted_iota(jnp.int32, (rows, 128), 1).astype(F32)
    row_index = lax.broadcasted_iota(jnp.int32, (rows, 128), 0).astype(F32)
    for tile in range(rows // 128):
        place = lane + float(tile * 128)
        seen = (place >= first) & (place <= row_index)
        bias_own[:, tile * 128:(tile + 1) * 128] = jnp.where(seen, 0.0, FLOOR_SCORE)

    head = jnp.broadcast_to(startb[0:1, :], (rows, 128))
    flags = jnp.where(
        lane == 0.0, jnp.where(first == head, 0.0, FLOOR_SCORE), jnp.where(lane == 1.0, 1.0, 0.0)
    ).astype(BF16)
    qx[0:rows, :] = flags
    qx[rows:2 * rows, :] = flags
    for slot, distance in enumerate(DISTANCE):
        hidden = jnp.where(row_index - float(distance * rows) >= head, 0.0, FLOOR_SCORE)
        kx[slot * rows:(slot + 1) * rows, :] = jnp.where(
            lane == 0.0, 1.0, jnp.where(lane == 1.0, hidden, 0.0)
        ).astype(BF16)

    def key_values(source, count):
        def column_tile(index, carry):
            cols = pl.ds(pl.multiple_of(index * TILE, TILE), TILE)
            normed = source()
            kb[0:count * rows, cols] = jnp.dot(
                normed, wk[:, cols], preferred_element_type=F32
            ).astype(BF16)
            vb[0:count * rows, cols] = jnp.dot(
                normed, wv[:, cols], preferred_element_type=F32
            ).astype(BF16)
            return carry

        lax.fori_loop(0, width // TILE, column_tile, 0)

    def attend(slot, count):
        keys = count * rows
        opening = slot is None

        def pair_step(pair, carry):
            cols = pl.ds(pl.multiple_of(pair * 128, 128), 128)
            query, key = q2[:, cols], kb[0:keys, cols]
            if not opening:
                query = jnp.concatenate([query, qx[...]], axis=1)
                key = jnp.concatenate([key, kx[slot * rows:slot * rows + keys, :]], axis=1)
            scores = lax.dot_general(
                query, key, (((1,), (1,)), ((), ())), preferred_element_type=F32
            )
            if opening:
                shade = bias_own[...]
                scores = scores + jnp.concatenate([shade, shade], axis=0)
            top = jnp.broadcast_to(
                jnp.max(scores, axis=-1, keepdims=True), (2 * rows, 128)
            )
            if not opening:
                before = mx[pair]
                top = jnp.maximum(top, before)
            weights16 = jnp.exp(scores - jnp.tile(top, (1, keys // 128))).astype(BF16)
            values = jnp.concatenate(
                [vb[0:keys, cols], jnp.ones((keys, 128), BF16)], axis=1
            )
            summed = jnp.dot(weights16, values, preferred_element_type=F32)
            if not opening:
                summed = summed + acc[pair] * jnp.tile(jnp.exp(before - top), (1, 2))
            acc[pair] = summed
            mx[pair] = top
            return carry

        lax.fori_loop(0, pairs, pair_step, 0, unroll=UNROLL)

    weights[0].wait()

    def query_tile(index, carry):
        cols = pl.ds(pl.multiple_of(index * 256, 256), 256)
        query = jnp.dot(own[...], wq[:, cols], preferred_element_type=F32)
        query = query.astype(BF16).astype(F32) * (HD ** -0.5)
        low = lax.broadcasted_iota(jnp.int32, (rows, 256), 1) % 128 < HD
        q2[0:rows, cols] = jnp.where(low, query, 0.0).astype(BF16)
        q2[rows:2 * rows, cols] = jnp.where(low, 0.0, query).astype(BF16)
        return carry

    lax.fori_loop(0, width // 256, query_tile, 0)
    weights[1].wait()
    weights[2].wait()
    key_values(lambda: own[...], 1)

    def relay_first(part):
        wait_here(B, part)
        start(D, part)
        start(H, part)
        wait_here(A, part)
        start(F, part)
        start(E, part)

    def relay_second(part):
        wait_here(F, part)
        start(I, part)
        start(G, part)

    attend(None, 1)
    for part in range(PIECES):
        relay_first(part)

    def remote(slot, count):
        key_values(
            lambda: xb[slot:slot + count].reshape(count * rows, width), count
        )
        attend(slot, count)

    for turn, (slot, count) in enumerate(GROUPS):
        if turn == len(GROUPS) - 2:
            for part in range(PIECES):
                relay_second(part)
        if turn == len(GROUPS) - 1:
            for event in (C, D, E, G, H, I):
                for part in range(PIECES):
                    wait_here(event, part)
        remote(slot, count)

    low = lax.broadcasted_iota(jnp.int32, (rows, 128), 1) < HD

    def close_pair(pair, carry):
        cols = pl.ds(pl.multiple_of(pair * 128, 128), 128)
        state = acc[pair]
        total = jnp.where(low, state[0:rows, 0:128], state[rows:2 * rows, 0:128])
        weight_sum = jnp.where(low, state[0:rows, 128:256], state[rows:2 * rows, 128:256])
        heads[:, cols] = (total / weight_sum).astype(BF16)
        return carry

    lax.fori_loop(0, pairs, close_pair, 0)
    weights[3].wait()

    def output_tile(index, carry):
        cols = pl.ds(pl.multiple_of(index * 256, 256), 256)
        res[:, cols] = (
            x_ref[:, cols].astype(F32)
            + jnp.dot(heads[...], wo[:, cols], preferred_element_type=F32)
        ).astype(BF16)
        return carry

    lax.fori_loop(0, width // 256, output_tile, 0)
    xn[0:rows, :] = layer_norm(res[...].astype(F32), nc_ref[...]).astype(BF16)
    weights[4].wait()

    def unit_tile(index, carry):
        cols = pl.ds(pl.multiple_of(index * 256, 256), 256)
        gate_cols = pl.ds(pl.multiple_of(width + index * 256, 256), 256)
        normed = xn[0:rows, :]
        value = jnp.dot(normed, wg[:, cols], preferred_element_type=F32)
        gate = jnp.dot(normed, wg[:, gate_cols], preferred_element_type=F32)
        gated = (value * jax.nn.sigmoid(gate)).astype(BF16)
        gb[:, cols] = gated
        gext[32:32 + rows, cols] = gated.astype(F32)
        return carry

    lax.fori_loop(0, width // 256, unit_tile, 0)

    rim = pltpu.make_async_remote_copy(
        src_ref=gb.at[pl.ds(rows - 32, 32)],
        dst_ref=halo,
        send_sem=halo_sem.at[0],
        recv_sem=halo_sem.at[1],
        device_id={"seq": me + 1},
        device_id_type=MESH,
    )

    @pl.when(me + 1 < n)
    def _():
        rim.start()

    chunk = 64

    def depth_tile(base, cols):
        back = (
            lax.broadcasted_iota(jnp.int32, (chunk, 128), 0).astype(F32) + float(base)
            - startb[pl.ds(base, chunk), :]
        )
        total = jnp.zeros((chunk, 128), F32)
        for tap in range(KW):
            piece_rows = gext[pl.ds(base + 2 + tap, chunk), cols]
            kept = jnp.where(back >= float(KW - 1 - tap), piece_rows, 0.0)
            total = total + kept * wd_ref[tap:tap + 1, cols]
        depth[pl.ds(base, chunk), cols] = total

    def interior(index, carry):
        cols = pl.ds(pl.multiple_of(index * 128, 128), 128)
        for base in range(chunk, rows, chunk):
            depth_tile(base, cols)
        return carry

    lax.fori_loop(0, pairs, interior, 0)

    def finish(low_row, count):
        normed_depth = layer_norm(depth[low_row:low_row + count, :], nd_ref[...])
        out_ref[low_row:low_row + count, :] = (
            res[low_row:low_row + count, :].astype(F32)
            + normed_depth * jax.nn.sigmoid(normed_depth)
        ).astype(BF16)

    finish(chunk, rows - chunk)

    @pl.when(me == 0)
    def _():
        halo[...] = jnp.zeros_like(halo)

    @pl.when(me > 0)
    def _():
        rim.wait_recv()

    gext[0:32, :] = halo[...].astype(F32)

    def edge(index, carry):
        depth_tile(0, pl.ds(pl.multiple_of(index * 128, 128), 128))
        return carry

    lax.fori_loop(0, pairs, edge, 0)
    finish(0, chunk)

    for event in range(9):
        for part in range(PIECES):
            wait_sent(event, part)

    @pl.when(me + 1 < n)
    def _():
        rim.wait_send()


def body(
    frames_in, rec_start, norm_attn, w_query, w_key, w_value, w_out, norm_conv, w_glu, w_depth,
    norm_depth,
):
    rows, width = frames_in.shape
    pairs = width // 128
    vmem = pl.BlockSpec(memory_space=pltpu.VMEM)
    hbm = pl.BlockSpec(memory_space=pl.ANY)
    square = pltpu.VMEM((width, width), BF16)
    return pl.pallas_call(
        kernel,
        out_shape=jax.ShapeDtypeStruct((rows, width), BF16),
        in_specs=[vmem] * 6 + [hbm] * 5,
        out_specs=vmem,
        scratch_shapes=[
            pltpu.VMEM((5, rows, width), BF16),
            pltpu.VMEM((rows, width), BF16),
            pltpu.VMEM((2 * rows, 128), BF16),
            pltpu.VMEM((5 * rows, 128), BF16),
            square, square, square, square,
            pltpu.VMEM((width, 2 * width), BF16),
            pltpu.VMEM((rows, width), BF16),
            pltpu.VMEM((2 * rows, width), BF16),
            pltpu.VMEM((3 * rows, width), BF16),
            pltpu.VMEM((3 * rows, width), BF16),
            pltpu.VMEM((rows, rows), F32),
            pltpu.VMEM((rows, 128), F32),
            pltpu.VMEM((pairs, 2 * rows, 128), F32),
            pltpu.VMEM((pairs, 2 * rows, 256), F32),
            pltpu.VMEM((rows, width), BF16),
            pltpu.VMEM((rows, width), BF16),
            pltpu.VMEM((rows, width), BF16),
            pltpu.VMEM((32, width), BF16),
            pltpu.VMEM((rows + 32, width), F32),
            pltpu.VMEM((rows, width), F32),
            pltpu.SemaphoreType.DMA((5,)),
            pltpu.SemaphoreType.DMA((9, PIECES)),
            pltpu.SemaphoreType.DMA((9, PIECES)),
            pltpu.SemaphoreType.DMA((2,)),
        ],
        compiler_params=pltpu.CompilerParams(
            collective_id=0, has_side_effects=True, vmem_limit_bytes=60 * 1024 * 1024
        ),
    )(
        frames_in, rec_start.reshape(1, rows), norm_attn.reshape(1, width),
        norm_conv.reshape(1, width), norm_depth.reshape(1, width), w_depth,
        w_query, w_key, w_value, w_out, w_glu,
    )


def solution(mesh):
    return jax.shard_map(
        body,
        mesh=mesh,
        in_specs=(P(("groups", "seq"), None), P(("groups", "seq"))) + (P(),) * 9,
        out_specs=P(("groups", "seq"), None),
        check_vma=False,
    )
```

```python
import jax
import jax.numpy as jnp
from jax import lax
from jax.experimental import pallas as pl
from jax.experimental.pallas import tpu as pltpu
from jax.sharding import PartitionSpec as P

HD = 64
KW = 31
EPSILON = 1e-05
FLOOR_SCORE = -1e30
F32 = jnp.float32
BF16 = jnp.bfloat16
MESH = pl.DeviceIdType.MESH
PIECES = 4
UNROLL = 8
TILE = 512
GROUPS = ((0, 1), (1, 1), (2, 2), (4, 1))
PLACE = {4: 0, 2: 1, 1: 2, 3: 3, 5: 4}
DISTANCE = (4, 2, 1, 3, 5)
A, B, C, D, E, F, G, H, I = range(9)


def layer_norm(entries, scaling):
    center = entries - jnp.mean(entries, axis=-1, keepdims=True)
    spread = jnp.mean(center * center, axis=-1, keepdims=True)
    return center * lax.rsqrt(spread + EPSILON) * scaling


def kernel(
    x_ref, start_ref, na_ref, nc_ref, nd_ref, wd_ref,
    wq_hbm, wk_hbm, wv_hbm, wo_hbm, wg_hbm,
    out_ref,
    xb, own, qx, kx, wq, wk, wv, wo, wg, xn, q2, kb, vb, bias_own, startb, mx, acc, heads,
    res, gb, halo, gext, depth,
    w_sem, send_sem, recv_sem, halo_sem,
):
    n = lax.axis_size("seq")
    me = lax.axis_index("seq")
    p = me % 4
    rows, width = x_ref.shape
    piece = rows // PIECES
    pairs = width // 128

    barrier = pltpu.get_barrier_semaphore()
    peers = jnp.int32(0)
    for delta in (-4, -3, -2, -1, 1, 2, 3, 4):
        inside = (me + delta >= 0) & (me + delta < n)
        peers = peers + jnp.where(inside, 1, 0)

        @pl.when(inside)
        def _():
            pl.semaphore_signal(
                barrier, inc=1, device_id={"seq": me + delta}, device_id_type=MESH
            )
    pl.semaphore_wait(barrier, peers)

    def move(event, part, source, target, distance):
        span = pl.ds(part * piece, piece)
        src = own.at[span] if source is None else xb.at[PLACE[source], span]
        return pltpu.make_async_remote_copy(
            src_ref=src,
            dst_ref=xb.at[PLACE[distance], span],
            send_sem=send_sem.at[event, part],
            recv_sem=recv_sem.at[event, part],
            device_id={"seq": target},
            device_id_type=MESH,
        )

    even = p % 2 == 0
    sends = {
        A: [(me + 4 < n, None, me + 4, 4)],
        B: [(p < 2, None, me + 2, 2)],
        C: [(even, None, me + 1, 1)],
        D: [(p == 2, 2, me + 1, 3), (p == 3, 2, me - 1, 1)],
        E: [((me >= 4) & even, 4, me + 1, 5), ((me >= 4) & (p % 2 == 1), 4, me - 1, 3)],
        F: [((me >= 4) & (p >= 2), 4, me - 2, 2)],
        G: [((me >= 4) & (p == 0), 2, me + 1, 3), ((me >= 4) & (p == 1), 2, me - 1, 1)],
        H: [((p == 3) & (me + 3 < n), 2, me + 3, 5)],
        I: [((me >= 4) & (p == 1) & (me + 3 < n), 2, me + 3, 5)],
    }
    receipts = {
        A: [(me >= 4, 4)],
        B: [(p >= 2, 2)],
        C: [(p % 2 == 1, 1)],
        D: [(p == 3, 3), (p == 2, 1)],
        E: [((me >= 4) & (p % 2 == 1), 5), ((me >= 4) & even, 3)],
        F: [((me >= 4) & (p < 2), 2)],
        G: [((me >= 4) & (p == 1), 3), ((me >= 4) & (p == 0), 1)],
        H: [((me >= 4) & (p == 2), 5)],
        I: [((me >= 8) & (p == 0), 5)],
    }

    def start(event, part):
        for condition, source, target, distance in sends[event]:
            @pl.when(condition)
            def _():
                move(event, part, source, target, distance).start()

    def wait_sent(event, part):
        for condition, source, target, distance in sends[event]:
            @pl.when(condition)
            def _():
                move(event, part, source, target, distance).wait_send()

    def wait_here(event, part):
        for condition, distance in receipts[event]:
            @pl.when(condition)
            def _():
                move(event, part, None, me, distance).wait_recv()

    weights = [
        pltpu.make_async_copy(src, dst, w_sem.at[index])
        for index, (src, dst) in enumerate(
            ((wq_hbm, wq), (wk_hbm, wk), (wv_hbm, wv), (wo_hbm, wo), (wg_hbm, wg))
        )
    ]
    for copy in weights:
        copy.start()

    gain = na_ref[...]
    for part in range(PIECES):
        own[part * piece:(part + 1) * piece, :] = layer_norm(
            x_ref[part * piece:(part + 1) * piece, :].astype(F32), gain
        ).astype(BF16)
        start(A, part)
        start(B, part)
    for part in range(PIECES):
        start(C, part)

    for distance in DISTANCE:
        @pl.when(me < distance)
        def _():
            xb[PLACE[distance]] = jnp.zeros((rows, width), BF16)

    column = jnp.broadcast_to(start_ref[...].astype(F32), (rows, rows)).T
    startb[...] = column[:, :128] - (me * rows).astype(F32)
    first = startb[...]
    lane = lax.broadcasted_iota(jnp.int32, (rows, 128), 1).astype(F32)
    row_index = lax.broadcasted_iota(jnp.int32, (rows, 128), 0).astype(F32)
    for tile in range(rows // 128):
        place = lane + float(tile * 128)
        seen = (place >= first) & (place <= row_index)
        bias_own[:, tile * 128:(tile + 1) * 128] = jnp.where(seen, 0.0, FLOOR_SCORE)

    head = jnp.broadcast_to(startb[0:1, :], (rows, 128))
    flags = jnp.where(
        lane == 0.0, jnp.where(first == head, 0.0, FLOOR_SCORE), jnp.where(lane == 1.0, 1.0, 0.0)
    ).astype(BF16)
    qx[0:rows, :] = flags
    qx[rows:2 * rows, :] = flags
    for slot, distance in enumerate(DISTANCE):
        hidden = jnp.where(row_index - float(distance * rows) >= head, 0.0, FLOOR_SCORE)
        kx[slot * rows:(slot + 1) * rows, :] = jnp.where(
            lane == 0.0, 1.0, jnp.where(lane == 1.0, hidden, 0.0)
        ).astype(BF16)

    def key_values(source, count):
        def column_tile(index, carry):
            cols = pl.ds(pl.multiple_of(index * TILE, TILE), TILE)
            normed = source()
            kb[0:count * rows, cols] = jnp.dot(
                normed, wk[:, cols], preferred_element_type=F32
            ).astype(BF16)
            vb[0:count * rows, cols] = jnp.dot(
                normed, wv[:, cols], preferred_element_type=F32
            ).astype(BF16)
            return carry

        lax.fori_loop(0, width // TILE, column_tile, 0)

    def attend(slot, count):
        keys = count * rows
        opening = slot is None

        def pair_step(pair, carry):
            cols = pl.ds(pl.multiple_of(pair * 128, 128), 128)
            query, key = q2[:, cols], kb[0:keys, cols]
            if not opening:
                query = jnp.concatenate([query, qx[...]], axis=1)
                key = jnp.concatenate([key, kx[slot * rows:slot * rows + keys, :]], axis=1)
            scores = lax.dot_general(
                query, key, (((1,), (1,)), ((), ())), preferred_element_type=F32
            )
            if opening:
                shade = bias_own[...]
                scores = scores + jnp.concatenate([shade, shade], axis=0)
            top = jnp.broadcast_to(
                jnp.max(scores, axis=-1, keepdims=True), (2 * rows, 128)
            )
            if not opening:
                before = mx[pair]
                top = jnp.maximum(top, before)
            weights16 = jnp.exp(scores - jnp.tile(top, (1, keys // 128))).astype(BF16)
            values = jnp.concatenate(
                [vb[0:keys, cols], jnp.ones((keys, 128), BF16)], axis=1
            )
            summed = jnp.dot(weights16, values, preferred_element_type=F32)
            if not opening:
                summed = summed + acc[pair] * jnp.tile(jnp.exp(before - top), (1, 2))
            acc[pair] = summed
            mx[pair] = top
            return carry

        lax.fori_loop(0, pairs, pair_step, 0, unroll=UNROLL)

    weights[0].wait()

    def query_tile(index, carry):
        cols = pl.ds(pl.multiple_of(index * 256, 256), 256)
        query = jnp.dot(own[...], wq[:, cols], preferred_element_type=F32)
        query = query.astype(BF16).astype(F32) * (HD ** -0.5)
        low = lax.broadcasted_iota(jnp.int32, (rows, 256), 1) % 128 < HD
        q2[0:rows, cols] = jnp.where(low, query, 0.0).astype(BF16)
        q2[rows:2 * rows, cols] = jnp.where(low, 0.0, query).astype(BF16)
        return carry

    lax.fori_loop(0, width // 256, query_tile, 0)
    weights[1].wait()
    weights[2].wait()
    key_values(lambda: own[...], 1)

    def relay_first(part):
        wait_here(B, part)
        start(D, part)
        start(H, part)
        wait_here(A, part)
        start(F, part)
        start(E, part)

    def relay_second(part):
        wait_here(F, part)
        start(I, part)
        start(G, part)

    relay_first(0)
    attend(None, 1)
    for part in range(1, PIECES):
        relay_first(part)

    def remote(slot, count):
        key_values(
            lambda: xb[slot:slot + count].reshape(count * rows, width), count
        )
        attend(slot, count)

    for turn, (slot, count) in enumerate(GROUPS):
        if turn == 1:
            for part in range(PIECES):
                relay_second(part)
        arrivals = {2: (C, D, E, G), 3: (H, I)} if len(GROUPS) == 4 else {2: (C, D, E, G, H, I)}
        if turn in arrivals:
            for event in arrivals[turn]:
                for part in range(PIECES):
                    wait_here(event, part)
        remote(slot, count)

    low = lax.broadcasted_iota(jnp.int32, (rows, 128), 1) < HD

    def close_pair(pair, carry):
        cols = pl.ds(pl.multiple_of(pair * 128, 128), 128)
        state = acc[pair]
        total = jnp.where(low, state[0:rows, 0:128], state[rows:2 * rows, 0:128])
        weight_sum = jnp.where(low, state[0:rows, 128:256], state[rows:2 * rows, 128:256])
        heads[:, cols] = (total / weight_sum).astype(BF16)
        return carry

    lax.fori_loop(0, pairs, close_pair, 0)
    weights[3].wait()

    def output_tile(index, carry):
        cols = pl.ds(pl.multiple_of(index * 256, 256), 256)
        res[:, cols] = (
            x_ref[:, cols].astype(F32)
            + jnp.dot(heads[...], wo[:, cols], preferred_element_type=F32)
        ).astype(BF16)
        return carry

    lax.fori_loop(0, width // 256, output_tile, 0)
    xn[0:rows, :] = layer_norm(res[...].astype(F32), nc_ref[...]).astype(BF16)
    weights[4].wait()

    def unit_tile(index, carry):
        cols = pl.ds(pl.multiple_of(index * 256, 256), 256)
        gate_cols = pl.ds(pl.multiple_of(width + index * 256, 256), 256)
        normed = xn[0:rows, :]
        value = jnp.dot(normed, wg[:, cols], preferred_element_type=F32)
        gate = jnp.dot(normed, wg[:, gate_cols], preferred_element_type=F32)
        gated = (value * jax.nn.sigmoid(gate)).astype(BF16)
        gb[:, cols] = gated
        gext[32:32 + rows, cols] = gated.astype(F32)
        return carry

    lax.fori_loop(0, width // 256, unit_tile, 0)

    rim = pltpu.make_async_remote_copy(
        src_ref=gb.at[pl.ds(rows - 32, 32)],
        dst_ref=halo,
        send_sem=halo_sem.at[0],
        recv_sem=halo_sem.at[1],
        device_id={"seq": me + 1},
        device_id_type=MESH,
    )

    @pl.when(me + 1 < n)
    def _():
        rim.start()

    chunk = 64

    def depth_tile(base, cols):
        back = (
            lax.broadcasted_iota(jnp.int32, (chunk, 128), 0).astype(F32) + float(base)
            - startb[pl.ds(base, chunk), :]
        )
        total = jnp.zeros((chunk, 128), F32)
        for tap in range(KW):
            piece_rows = gext[pl.ds(base + 2 + tap, chunk), cols]
            kept = jnp.where(back >= float(KW - 1 - tap), piece_rows, 0.0)
            total = total + kept * wd_ref[tap:tap + 1, cols]
        depth[pl.ds(base, chunk), cols] = total

    def interior(index, carry):
        cols = pl.ds(pl.multiple_of(index * 128, 128), 128)
        for base in range(chunk, rows, chunk):
            depth_tile(base, cols)
        return carry

    lax.fori_loop(0, pairs, interior, 0)

    def finish(low_row, count):
        normed_depth = layer_norm(depth[low_row:low_row + count, :], nd_ref[...])
        out_ref[low_row:low_row + count, :] = (
            res[low_row:low_row + count, :].astype(F32)
            + normed_depth * jax.nn.sigmoid(normed_depth)
        ).astype(BF16)

    finish(chunk, rows - chunk)

    @pl.when(me == 0)
    def _():
        halo[...] = jnp.zeros_like(halo)

    @pl.when(me > 0)
    def _():
        rim.wait_recv()

    gext[0:32, :] = halo[...].astype(F32)

    def edge(index, carry):
        depth_tile(0, pl.ds(pl.multiple_of(index * 128, 128), 128))
        return carry

    lax.fori_loop(0, pairs, edge, 0)
    finish(0, chunk)

    for event in range(9):
        for part in range(PIECES):
            wait_sent(event, part)

    @pl.when(me + 1 < n)
    def _():
        rim.wait_send()


def body(
    frames_in, rec_start, norm_attn, w_query, w_key, w_value, w_out, norm_conv, w_glu, w_depth,
    norm_depth,
):
    rows, width = frames_in.shape
    pairs = width // 128
    vmem = pl.BlockSpec(memory_space=pltpu.VMEM)
    hbm = pl.BlockSpec(memory_space=pl.ANY)
    square = pltpu.VMEM((width, width), BF16)
    return pl.pallas_call(
        kernel,
        out_shape=jax.ShapeDtypeStruct((rows, width), BF16),
        in_specs=[vmem] * 6 + [hbm] * 5,
        out_specs=vmem,
        scratch_shapes=[
            pltpu.VMEM((5, rows, width), BF16),
            pltpu.VMEM((rows, width), BF16),
            pltpu.VMEM((2 * rows, 128), BF16),
            pltpu.VMEM((5 * rows, 128), BF16),
            square, square, square, square,
            pltpu.VMEM((width, 2 * width), BF16),
            pltpu.VMEM((rows, width), BF16),
            pltpu.VMEM((2 * rows, width), BF16),
            pltpu.VMEM((3 * rows, width), BF16),
            pltpu.VMEM((3 * rows, width), BF16),
            pltpu.VMEM((rows, rows), F32),
            pltpu.VMEM((rows, 128), F32),
            pltpu.VMEM((pairs, 2 * rows, 128), F32),
            pltpu.VMEM((pairs, 2 * rows, 256), F32),
            pltpu.VMEM((rows, width), BF16),
            pltpu.VMEM((rows, width), BF16),
            pltpu.VMEM((rows, width), BF16),
            pltpu.VMEM((32, width), BF16),
            pltpu.VMEM((rows + 32, width), F32),
            pltpu.VMEM((rows, width), F32),
            pltpu.SemaphoreType.DMA((5,)),
            pltpu.SemaphoreType.DMA((9, PIECES)),
            pltpu.SemaphoreType.DMA((9, PIECES)),
            pltpu.SemaphoreType.DMA((2,)),
        ],
        compiler_params=pltpu.CompilerParams(
            collective_id=0, has_side_effects=True, vmem_limit_bytes=60 * 1024 * 1024
        ),
    )(
        frames_in, rec_start.reshape(1, rows), norm_attn.reshape(1, width),
        norm_conv.reshape(1, width), norm_depth.reshape(1, width), w_depth,
        w_query, w_key, w_value, w_out, w_glu,
    )


def solution(mesh):
    return jax.shard_map(
        body,
        mesh=mesh,
        in_specs=(P(("groups", "seq"), None), P(("groups", "seq"))) + (P(),) * 9,
        out_specs=P(("groups", "seq"), None),
        check_vma=False,
    )
```
